128 devices in a mesh: sec: 2 (over core), blk: 64 (over z, x, y).
Axes of the slice: x: 4, y: 4, z: 4, core: 2. Of those that a mesh axis runs over, the one named last changes fastest.
Arguments:
- state: float32 [2, 4, 16, 131072], P('sec', None, None, 'blk'), may hold values from -6 to 6
- neighbour: int32 [2, 6, 131072], P('sec', None, 'blk'), may hold values from 0 to 2303, as said below
- edge_weight: float32 [2, 6, 131072], P('sec', None, 'blk'), may hold values from 0.02 to 0.15
- coupling_rate: float32 [2, 4, 131072], P('sec', None, 'blk'), may hold values from 0.05 to 0.5
- vertical_mix: float32 [2, 4, 16, 16], P('sec'), may hold values from -1 to 2, as said below
- remap_source: int32 [2, 524288], P('sec', 'blk'), may hold values from 0 to 2047
- remap_owner: int32 [2, 524288, 1], P('sec', 'blk'), may hold values from 0 to 63; in each aligned block of 8192 rows (0 to 8191, 8192 to 16383, ..., all dimensions but the last counted through in order) at most 256 rows name the same one
- remap_cell: int32 [2, 524288], P('sec', 'blk'), may hold values from 0 to 2047
- remap_weight: float32 [2, 524288], P('sec', 'blk'), may hold values from 0.1 to 0.6
Outputs:
- new_state: float32 [2, 4, 16, 131072], P('sec', None, None, 'blk')
- remapped: float32 [2, 4, 131072], P('sec', None, 'blk')
The draws below stay inside these ranges and needn't reach their ends.
Inputs may be any that keep to these rules, and one draw needn't show every extreme that they name: Entry (s, k, c) is the position of neighbour k of cell c in c's block extended by 128 cells on each side: positions below 128 are the previous block's last cells, then the own block, then the next block's first cells; blocks wrap around. `vertical_mix`: each inverse is an identity-dominated dense matrix. `remap_source`: entries of a block name source cells of that same block. `remap_owner`: among the 8192 rows of one block no destination block is named by more than 256 rows; some block names one destination exactly 256 times.
All inputs are finite; a program needn't handle non-finite values.
Results may differ from the reference program's by a relative error of at most 0.0001.
Values sent between devices are 32-bit elements; how exact they have to be, the bound alone decides.
No kernel may reach another device: no remote copies, remote signals or barrier semaphores. Data moves between devices by JAX's collectives and lax.ppermute only.
A program may use at most 128 MiB of HBM per device.

```python
import math
import jax
import jax.numpy as jnp
import numpy as np
from jax import lax

F = 4
K = 6
LEV = 16
CELLS_DEV = 2048
SUB = 4
RIM = 128
E_DEV = 8192
CAP = 256
CELLS = 131072
ENTRIES = 524288
N_BLK = 64


def draw_neighbour(key, part):
    shape = (2, K, CELLS)
    local = lax.broadcasted_iota(jnp.int32, shape, 2) % CELLS_DEV
    offset = jax.random.randint(key, shape, -RIM, RIM + 1)
    return (local + RIM + offset).astype(jnp.int32)


def draw_vertical_mix(key, part):
    shape = (2, F, LEV, LEV)
    noise = jnp.clip(jax.random.normal(key, shape, jnp.float32), -4.0, 4.0)
    rows = lax.broadcasted_iota(jnp.int32, shape, 2)
    columns = lax.broadcasted_iota(jnp.int32, shape, 3)
    identity = (rows == columns).astype(jnp.float32)
    return 0.7 * identity + 0.3 / math.sqrt(LEV) * noise


def place_ends(entries, rng, smallest, high):
    shape = entries.shape
    place = [jax.random.randint(jax.random.fold_in(rng, axis), (), 0, shape[axis]) for axis in range(len(shape))]
    entries = entries.at[tuple(place)].set(smallest)
    longest = shape.index(max(shape))
    place[longest] = (place[longest] + 1) % shape[longest]
    return entries.at[tuple(place)].set(high)


def block_levels(own_key, extent, shards, least, largest):
    factor_of, own = 1.0, jax.random.fold_in(own_key, 6)
    for dim, blocks in shards:
        steps = jnp.exp(jax.random.uniform(jax.random.fold_in(own, dim), (blocks,), jnp.float32, least / len(shards), largest / len(shards)))
        factor_of = factor_of * jnp.repeat(steps, extent[dim] // blocks).reshape([-1 if axis == dim else 1 for axis in range(len(extent))])
    return factor_of


def routed_block(rng, own, number, rows, amount, top, reach, skew):
    sequence = jax.random.permutation(rng, amount)
    packed, common = shares(amount, rows * top, reach, skew, True), shares(amount, rows * top, reach, skew, False)
    places = jnp.arange(amount)

    def named(tallies, rotation):
        used = int((tallies > 0).sum())
        fixed = max(1, used // 4)
        shifted = fixed + (places - fixed + rotation * (used - fixed)) % max(1, amount - fixed)
        return jnp.zeros((amount,), jnp.int32).at[sequence[jnp.where(places < fixed, places, shifted)]].set(jnp.asarray(tallies, jnp.int32))

    tallies = jnp.where(number % 4 == 0, named(packed, number // 4), named(common, number - number // 4 - 1))
    mixed = jax.random.permutation(jax.random.fold_in(own, 3), amount)
    giver, sink = mixed[0:amount // 2 * 2:2], mixed[1:amount // 2 * 2:2]
    slack = jnp.minimum(tallies[giver] - 1, reach - tallies[sink]) // 2
    slack = jnp.where((giver == sequence[0]) | (sink == sequence[0]) | (tallies[sink] == 0), 0, jnp.maximum(slack, 0))
    shifted = jax.random.randint(jax.random.fold_in(own, 4), (amount // 2,), 0, 1 << 20) % (slack + 1)
    tallies = tallies.at[giver].add(-shifted).at[sink].add(shifted)
    items = jnp.searchsorted(jnp.cumsum(tallies), jnp.arange(rows * top), side="right").astype(jnp.int32)
    listing = items.reshape(top, rows).T
    listing = listing[jax.random.permutation(jax.random.fold_in(own, 1), rows)]
    rotation = jax.random.randint(jax.random.fold_in(own, 2), (rows, 1), 0, top)
    return jnp.take_along_axis(listing, (jnp.arange(top)[None, :] + rotation) % top, axis=1)


def shares(amount, total, most, slope, full):
    loads = [(1 << 20) // math.isqrt(standing ** slope) + 1 for standing in range(1, amount + 1)]
    largest = most if full else min(most, max(-(-total // amount), total * loads[0] // sum(loads)))
    least = 1 if total - largest >= amount - 1 else 0
    counts, surplus = [largest] + [least] * (amount - 1), total - largest - least * (amount - 1)
    while surplus > 0:
        candidates = [i for i in range(1, amount) if counts[i] < largest] or [i for i in range(1, amount) if counts[i] < most]
        pool, left = sum([loads[i] for i in candidates]), surplus
        for i in candidates:
            extra = min(most - counts[i], max(1, left * loads[i] // pool), surplus)
            counts[i] = counts[i] + extra
            surplus = surplus - extra
    return np.array(counts)


def bell_draw(key, dims, width, limit, pieces=(), kind=jnp.bfloat16):
    drawn = jax.random.normal(key, dims, jnp.float32) * width
    if len(pieces) > 0:
        drawn = block_levels(key, dims, pieces, -0.22, 0.18) * drawn
    return jnp.clip(drawn, min=-limit, max=limit).astype(kind)


def setup_inputs(seed: int = 0) -> dict:
    key_list = jax.random.split(jax.random.key(seed), 10)
    state = bell_draw(key_list[0], (2, F, LEV, CELLS), 1.0, 6.0, ((0, 2), (3, 64)), jnp.float32)
    neighbour = draw_neighbour(jax.random.fold_in(key_list[9], 71), 0)
    edge_weight = jnp.clip(jnp.exp(math.log(0.15) - 2.014903 * jax.random.uniform(key_list[2], (2, K, CELLS), jnp.float32) ** block_levels(key_list[2], (2, K, CELLS), ((0, 2), (2, 64)), -0.2, 0.2)), 0.02, 0.15)
    coupling_rate = jnp.clip(jnp.exp(math.log(0.5) - 2.3025851 * jax.random.uniform(key_list[3], (2, F, CELLS), jnp.float32) ** block_levels(key_list[3], (2, F, CELLS), ((0, 2), (2, 64)), -0.2, 0.2)), 0.05, 0.5)
    vertical_mix = draw_vertical_mix(jax.random.fold_in(key_list[9], 71), 0)
    remap_source = place_ends(jax.random.randint(key_list[5], (2, ENTRIES), 0, CELLS_DEV), jax.random.fold_in(key_list[5], 1), 0, CELLS_DEV - 1).astype(jnp.int32)
    remap_owner_keys = jax.random.split(jax.random.fold_in(key_list[6], 1), 2 * ENTRIES // E_DEV)
    remap_owner_turns = jax.random.permutation(jax.random.fold_in(key_list[6], 3), 2 * ENTRIES // E_DEV)
    remap_owner = jax.vmap(lambda own, number: routed_block(jax.random.fold_in(key_list[6], 2), own, number, E_DEV, N_BLK, 1, CAP, 2))(remap_owner_keys, remap_owner_turns).reshape((2, ENTRIES, 1))
    remap_cell = place_ends(jax.random.randint(key_list[7], (2, ENTRIES), 0, CELLS_DEV), jax.random.fold_in(key_list[7], 1), 0, CELLS_DEV - 1).astype(jnp.int32)
    remap_weight = jnp.clip(0.1 + 0.5 * jax.random.uniform(key_list[8], (2, ENTRIES), jnp.float32) ** block_levels(key_list[8], (2, ENTRIES), ((0, 2), (1, 64)), -0.2, 0.2), 0.1, 0.6)
    return dict(state=state, neighbour=neighbour, edge_weight=edge_weight, coupling_rate=coupling_rate, vertical_mix=vertical_mix, remap_source=remap_source, remap_owner=remap_owner, remap_cell=remap_cell, remap_weight=remap_weight)


def reference(state, neighbour, edge_weight, coupling_rate, vertical_mix, remap_source, remap_owner, remap_cell, remap_weight):
    total_cells = CELLS_DEV * N_BLK
    rows = jnp.arange(E_DEV * N_BLK, dtype=jnp.int32)
    gathered = []
    for section in range(2):
        surface = state[section, :, 0, :]
        source_index = (rows // E_DEV) * CELLS_DEV + remap_source[section]
        contribution = remap_weight[section][None, :] * surface[:, source_index]
        dest_index = remap_owner[section, :, 0] * CELLS_DEV + remap_cell[section]
        gathered.append(jnp.zeros((F, total_cells), jnp.float32).at[:, dest_index].add(contribution))
    remapped = jnp.stack([gathered[1], gathered[0]])
    cells = jnp.arange(total_cells, dtype=jnp.int32)
    block_base = (cells // CELLS_DEV) * CELLS_DEV - RIM
    results = []
    for section in range(2):
        mixed = state[section]
        for step in range(SUB):
            update = jnp.zeros_like(mixed)
            for slot in range(K):
                target = (block_base + neighbour[section, slot]) % total_cells
                update = update + edge_weight[section, slot] * (mixed[:, :, target] - mixed)
            mixed = mixed + update
        surface_top = mixed[:, 0, :] + coupling_rate[section] * (remapped[section] - mixed[:, 0, :])
        forced = mixed.at[:, 0, :].set(surface_top)
        results.append(jnp.einsum('fij,fjc->fic', vertical_mix[section], forced, precision=lax.Precision.HIGHEST))
    return jnp.stack(results), remapped
```

```python
import jax
import jax.numpy as jnp
from jax import lax
from jax.experimental import pallas as pl
from jax.experimental.pallas import tpu as pltpu
from jax.sharding import PartitionSpec as P

SUB = 4
RIM = 128
LANE = 128
BF = jnp.bfloat16
F32 = jnp.float32
VMEM = pltpu.VMEM


def dot(a, b):
    return jnp.dot(a, b, preferred_element_type=F32)


def dot_nt(a, b):
    return lax.dot_general(a, b, (((1,), (1,)), ((), ())), preferred_element_type=F32)


def split(x):
    hi = x.astype(BF)
    lo = (x - hi.astype(F32)).astype(BF)
    return hi, lo


def build_kernel(nbr_ref, w_ref, hi_ref, lo_ref, diag_ref):
    slots, width = nbr_ref.shape
    rows = hi_ref.shape[0]
    cells = rows - 2 * RIM
    pos, wgt = [], []
    for k in range(slots):
        p = nbr_ref[k : k + 1, :]
        p = jnp.where(p < RIM, p + cells, jnp.where(p < cells + RIM, p - RIM, p))
        pos.append(p)
        wgt.append(w_ref[k : k + 1, :])
    total = wgt[0]
    for k in range(1, slots):
        total = total + wgt[k]
    diag_ref[...] = 1.0 - total
    for k in range(1, slots):
        for j in range(k):
            same = pos[j] == pos[k]
            wgt[j] = jnp.where(same, wgt[j] + wgt[k], wgt[j])
            pos[k] = jnp.where(same, -1, pos[k])
    step = 32
    whi, wlo = [], []
    for k in range(slots):
        hi = wgt[k].astype(BF).astype(F32)
        whi.append(jnp.broadcast_to(hi, (step, width)).astype(BF))
        wlo.append(jnp.broadcast_to(wgt[k] - hi, (step, width)).astype(BF))
    for block in range(rows // 256):
        loc = []
        for k in range(slots):
            local = pos[k] - block * 256
            local = jnp.where((local >= 0) & (local < 256), local, -1).astype(F32)
            loc.append(jnp.broadcast_to(local, (step, width)).astype(BF))
        for part in range(256 // step):
            row = (lax.broadcasted_iota(jnp.int32, (step, width), 0) + part * step).astype(F32).astype(BF)
            hi = jnp.zeros((step, width), BF)
            lo = jnp.zeros((step, width), BF)
            for k in range(slots):
                here = row == loc[k]
                hi = jnp.where(here, whi[k], hi)
                lo = jnp.where(here, wlo[k], lo)
            at = pl.ds(block * 256 + part * step, step)
            hi_ref[at, :] = hi
            lo_ref[at, :] = lo


def build(nbr, w):
    slots, cells = nbr.shape
    rows = cells + 2 * RIM
    width = 128
    return pl.pallas_call(
        build_kernel,
        grid=(cells // width,),
        in_specs=[pl.BlockSpec((slots, width), lambda i: (0, i))] * 2,
        out_specs=[
            pl.BlockSpec((rows, width), lambda i: (0, i)),
            pl.BlockSpec((rows, width), lambda i: (0, i)),
            pl.BlockSpec((1, width), lambda i: (0, i)),
        ],
        out_shape=[
            jax.ShapeDtypeStruct((rows, cells), BF),
            jax.ShapeDtypeStruct((rows, cells), BF),
            jax.ShapeDtypeStruct((1, cells), F32),
        ],
        name="build",
    )(nbr, w)


def own_kernel(x_ref, hi_ref, lo_ref, diag_ref, out_ref, cat_ref):
    columns = x_ref.shape[0]
    width = out_ref.shape[1]

    @pl.when(pl.program_id(0) == 0)
    def _():
        hi, lo = split(x_ref[...])
        cat_ref[0:columns, :] = hi
        cat_ref[columns:, :] = lo

    both = dot(cat_ref[...], hi_ref[...])
    low = dot(cat_ref[0:columns, :], lo_ref[...])
    at = pl.ds(pl.multiple_of(pl.program_id(0) * width, width), width)
    out_ref[...] = diag_ref[...] * x_ref[:, at] + (both[0:columns] + both[columns:] + low)


def own(x, a_hi, a_lo, diag):
    columns, cells = x.shape
    width = 256
    return pl.pallas_call(
        own_kernel,
        grid=(cells // width,),
        in_specs=[
            pl.BlockSpec((columns, cells), lambda i: (0, 0)),
            pl.BlockSpec((cells, width), lambda i: (0, i)),
            pl.BlockSpec((cells, width), lambda i: (0, i)),
            pl.BlockSpec((1, width), lambda i: (0, i)),
        ],
        out_specs=pl.BlockSpec((columns, width), lambda i: (0, i)),
        out_shape=jax.ShapeDtypeStruct((columns, cells), F32),
        scratch_shapes=[VMEM((2 * columns, cells), BF)],
        name="own",
    )(x, a_hi, a_lo, diag)


def rim_update(part, low_ref, high_ref, hi_ref, lo_ref):
    columns = low_ref.shape[0]
    lo_hi, lo_lo = split(low_ref[...])
    hi_hi, hi_lo = split(high_ref[...])
    top = jnp.concatenate([lo_hi, hi_hi], axis=1)
    rest = jnp.concatenate([lo_lo, hi_lo], axis=1)
    both = dot(jnp.concatenate([top, rest], axis=0), hi_ref[...])
    return part + (both[0:columns] + both[columns:] + dot(top, lo_ref[...]))


def rim_kernel(part_ref, low_ref, high_ref, hi_ref, lo_ref, out_ref, first_ref, last_ref):
    out = rim_update(part_ref[...], low_ref, high_ref, hi_ref, lo_ref)
    out_ref[...] = out
    first_ref[...] = out[:, 0:RIM]
    last_ref[...] = out[:, out.shape[1] - RIM :]


def rim(part, low, high, a_hi, a_lo):
    columns, cells = part.shape
    last = cells // (2 * RIM)
    return pl.pallas_call(
        rim_kernel,
        grid=(1,),
        in_specs=[
            pl.BlockSpec((columns, cells), lambda i: (0, 0)),
            pl.BlockSpec((columns, RIM), lambda i: (0, 0)),
            pl.BlockSpec((columns, RIM), lambda i: (0, 0)),
            pl.BlockSpec((2 * RIM, cells), lambda i: (last, 0)),
            pl.BlockSpec((2 * RIM, cells), lambda i: (last, 0)),
        ],
        out_specs=[
            pl.BlockSpec((columns, cells), lambda i: (0, 0)),
            pl.BlockSpec((columns, RIM), lambda i: (0, 0)),
            pl.BlockSpec((columns, RIM), lambda i: (0, 0)),
        ],
        out_shape=[
            jax.ShapeDtypeStruct((columns, cells), F32),
            jax.ShapeDtypeStruct((columns, RIM), F32),
            jax.ShapeDtypeStruct((columns, RIM), F32),
        ],
        name="rim",
    )(part, low, high, a_hi, a_lo)


def finish_kernel(
    part_ref, low_ref, high_ref, hi_ref, lo_ref, remapped_ref, rate_ref, mix_ref, out_ref
):
    mixed = rim_update(part_ref[...], low_ref, high_ref, hi_ref, lo_ref)
    fields, levels = mix_ref.shape[0], mix_ref.shape[1]
    for f in range(fields):
        own_levels = mixed[f * levels : (f + 1) * levels]
        top = own_levels[0:1]
        top = top + rate_ref[f : f + 1, :] * (remapped_ref[f : f + 1, :] - top)
        row = lax.broadcasted_iota(jnp.int32, own_levels.shape, 0)
        forced = jnp.where(row == 0, jnp.broadcast_to(top, own_levels.shape), own_levels)
        out_ref[f] = jnp.dot(
            mix_ref[f], forced, preferred_element_type=F32, precision=lax.Precision.HIGHEST
        )


def finish(part, low, high, a_hi, a_lo, remapped, rate, mix):
    columns, cells = part.shape
    fields, levels = mix.shape[0], mix.shape[1]
    last = cells // (2 * RIM)
    return pl.pallas_call(
        finish_kernel,
        grid=(1,),
        in_specs=[
            pl.BlockSpec((columns, cells), lambda i: (0, 0)),
            pl.BlockSpec((columns, RIM), lambda i: (0, 0)),
            pl.BlockSpec((columns, RIM), lambda i: (0, 0)),
            pl.BlockSpec((2 * RIM, cells), lambda i: (last, 0)),
            pl.BlockSpec((2 * RIM, cells), lambda i: (last, 0)),
            pl.BlockSpec((fields, cells), lambda i: (0, 0)),
            pl.BlockSpec((fields, cells), lambda i: (0, 0)),
            pl.BlockSpec((fields, levels, levels), lambda i: (0, 0, 0)),
        ],
        out_specs=pl.BlockSpec((fields, levels, cells), lambda i: (0, 0, 0)),
        out_shape=jax.ShapeDtypeStruct((fields, levels, cells), F32),
        name="finish",
    )(part, low, high, a_hi, a_lo, remapped, rate, mix)


def pack_kernel(
    surface_ref, source_ref, owner_ref, cell_ref, weight_ref,
    vals_ref, cells_ref,
    tiles_ref, half_ref, slot_ref, hot_ref, left_ref, cleft_ref, right_ref, acc_ref, cacc_ref,
):
    fields = surface_ref.shape[0]
    rows = source_ref.shape[0]
    blocks = cells_ref.shape[0] // 2
    chunk = right_ref.shape[1]
    per = chunk // LANE
    source = source_ref[...]
    line, lane = source // LANE, source % LANE
    vals = []
    for f in range(fields):
        got = jnp.zeros((rows, LANE), F32)
        for h in range(surface_ref.shape[1] // LANE):
            table = jnp.broadcast_to(surface_ref[f : f + 1, h * LANE : (h + 1) * LANE], (rows, LANE))
            one = jnp.take_along_axis(table, lane, axis=1, mode="promise_in_bounds")
            got = jnp.where(line == h, one, got)
        vals.append(got * weight_ref[...])
    owner_row = lax.broadcasted_iota(jnp.int32, (blocks, LANE), 0)
    i0 = lax.broadcasted_iota(jnp.int32, (LANE, LANE), 0)
    i1 = lax.broadcasted_iota(jnp.int32, (LANE, LANE), 1)
    before = (i0 < i1).astype(F32).astype(BF)
    for r in range(rows):
        hot = (owner_row == owner_ref[r : r + 1, :]).astype(F32)
        hot_ref[r * blocks : (r + 1) * blocks, :] = hot.astype(BF)
    prefix = dot(hot_ref[...], before)
    base = jnp.zeros((blocks, 1), F32)
    for r in range(rows):
        hot = hot_ref[r * blocks : (r + 1) * blocks, :].astype(F32)
        rank = jnp.sum(hot * (prefix[r * blocks : (r + 1) * blocks] + base), axis=0, keepdims=True)
        slot_ref[r : r + 1, :] = rank.astype(jnp.int32)
        base = base + jnp.sum(hot, axis=1, keepdims=True)
    slot = slot_ref[...]
    half = slot // LANE
    slot_ref[...] = slot % LANE
    for h in range(2):
        for f in range(fields):
            tiles_ref[pl.ds(h * fields + f, rows, stride=2 * fields), :] = jnp.where(
                half == h, vals[f], 0.0
            )
    cell = cell_ref[...]
    for part, piece in enumerate(((cell // 16) * 16, cell % 16)):
        for h in range(2):
            half_ref[pl.ds(part * 2 + h, rows, stride=4), :] = jnp.where(
                half == h, piece, 0
            ).astype(F32)

    acc_ref[...] = jnp.zeros_like(acc_ref)
    cacc_ref[...] = jnp.zeros_like(cacc_ref)

    def body(c, _):
        for t in range(per):
            r = c * per + t
            at = pl.ds(t * LANE, LANE)
            tile = tiles_ref[pl.ds(pl.multiple_of(r * 8, 8), 8), :]
            hi = tile.astype(BF).astype(F32)
            tile = jnp.concatenate([hi, tile - hi], axis=0).astype(BF)
            who = jnp.broadcast_to(owner_ref[pl.ds(r, 1), :].astype(F32), (16, LANE)).astype(BF)
            zero = jnp.zeros((16, LANE), BF)
            for o in range(blocks):
                left_ref[o * 16 : (o + 1) * 16, at] = jnp.where(who == o, tile, zero)
            who = jnp.broadcast_to(owner_ref[pl.ds(r, 1), :], (2 * blocks, LANE))
            row = lax.broadcasted_iota(jnp.int32, (2 * blocks, LANE), 0)
            for part in range(2):
                a = jnp.broadcast_to(half_ref[pl.ds(r * 4 + part * 2, 1), :], (2 * blocks, LANE))
                b = jnp.broadcast_to(half_ref[pl.ds(r * 4 + part * 2 + 1, 1), :], (2 * blocks, LANE))
                picked = jnp.where(row % 2 == 0, a, b)
                cleft_ref[part * 2 * blocks : (part + 1) * 2 * blocks, at] = jnp.where(
                    row // 2 == who, picked, 0.0
                ).astype(BF)
            lanes = jnp.broadcast_to(slot_ref[pl.ds(r, 1), :], (LANE, LANE))
            right_ref[:, at] = (i0 == lanes).astype(F32).astype(BF)
        acc_ref[...] += dot_nt(left_ref[...], right_ref[...])
        cacc_ref[...] += dot_nt(cleft_ref[...], right_ref[...])
        return 0

    lax.fori_loop(0, rows // per, body, 0)
    for o in range(blocks):
        vals_ref[o * 8 : (o + 1) * 8, :] = acc_ref[o * 16 : o * 16 + 8, :] + acc_ref[o * 16 + 8 : o * 16 + 16, :]
    cells_ref[...] = cacc_ref[0 : 2 * blocks, :] + cacc_ref[2 * blocks :, :]


def pack(surface, source, owner, cell, weight, blocks):
    fields = surface.shape[0]
    rows = source.shape[0]
    chunk = 512
    return pl.pallas_call(
        pack_kernel,
        in_specs=[pl.BlockSpec(memory_space=VMEM)] * 5,
        out_specs=[pl.BlockSpec(memory_space=VMEM)] * 2,
        out_shape=[
            jax.ShapeDtypeStruct((blocks * 8, LANE), F32),
            jax.ShapeDtypeStruct((blocks * 2, LANE), F32),
        ],
        scratch_shapes=[
            VMEM((rows * 2 * fields, LANE), F32),
            VMEM((rows * 4, LANE), F32),
            VMEM((rows, LANE), jnp.int32),
            VMEM((rows * blocks, LANE), BF),
            VMEM((blocks * 16, chunk), BF),
            VMEM((blocks * 4, chunk), BF),
            VMEM((LANE, chunk), BF),
            VMEM((blocks * 16, LANE), F32),
            VMEM((blocks * 4, LANE), F32),
        ],
        name="pack",
    )(surface, source, owner, cell, weight)


def unpack_kernel(vals_ref, cells_ref, out_ref, left_ref, right_ref):
    fields, cells = out_ref.shape
    rows = cells_ref.shape[0]
    groups = cells // 256
    chunk = right_ref.shape[1]
    per = chunk // LANE
    r256 = lax.broadcasted_iota(jnp.int32, (256, LANE), 0)

    def body(c, acc):
        for t in range(per):
            r = c * per + t
            at = pl.ds(t * LANE, LANE)
            cell = cells_ref[pl.ds(r, 1), :].astype(jnp.int32)
            group, local = cell // 256, cell % 256
            vals = vals_ref[pl.ds(pl.multiple_of(r * fields, fields), fields), :]
            hi = vals.astype(BF).astype(F32)
            tile = jnp.concatenate([hi, vals - hi], axis=0)
            for g in range(groups):
                picked = jnp.where(jnp.broadcast_to(group, tile.shape) == g, tile, 0.0)
                left_ref[g * 8 : (g + 1) * 8, at] = picked
            right_ref[:, at] = (r256 == jnp.broadcast_to(local, (256, LANE))).astype(F32).astype(BF)
        return acc + dot_nt(left_ref[...].astype(BF), right_ref[...])

    acc = lax.fori_loop(0, rows // per, body, jnp.zeros((groups * 8, 256), F32))
    for g in range(groups):
        out_ref[:, g * 256 : (g + 1) * 256] = (
            acc[g * 8 : g * 8 + fields] + acc[g * 8 + fields : g * 8 + 2 * fields]
        )


def unpack(vals, cells, count):
    fields = vals.shape[0] // cells.shape[0]
    chunk = 1024
    return pl.pallas_call(
        unpack_kernel,
        in_specs=[pl.BlockSpec(memory_space=VMEM)] * 2,
        out_specs=pl.BlockSpec(memory_space=VMEM),
        out_shape=jax.ShapeDtypeStruct((fields, count), F32),
        scratch_shapes=[
            VMEM((count // 256 * 8, chunk), F32),
            VMEM((256, chunk), BF),
        ],
        name="unpack",
    )(vals, cells)


def per_device(
    state, neighbour, edge_weight, coupling_rate, vertical_mix,
    remap_source, remap_owner, remap_cell, remap_weight,
):
    fields, levels, cells = state.shape[1:]
    columns = fields * levels
    blocks = lax.axis_size("blk")
    forward = [(i, (i + 1) % blocks) for i in range(blocks)]
    backward = [(b, a) for a, b in forward]

    def lines(x):
        return x.reshape(-1, LANE)

    def exchange(first, last):
        low = lax.ppermute(last, "blk", forward)
        high = lax.ppermute(first, "blk", backward)
        return low, high

    x = state.reshape(columns, cells)
    halo = exchange(x[:, :RIM], x[:, cells - RIM :])
    vals, dest = pack(
        state[0, :, 0, :], lines(remap_source), lines(remap_owner), lines(remap_cell),
        lines(remap_weight), blocks,
    )
    vals = lax.all_to_all(vals.reshape(blocks, 8, LANE), "blk", 0, 0, tiled=True).reshape(-1, LANE)
    dest = lax.all_to_all(dest.reshape(blocks, 2, LANE), "blk", 0, 0, tiled=True).reshape(-1, LANE)
    a_hi, a_lo, diag = build(neighbour[0], edge_weight[0])
    for step in range(SUB - 1):
        part = own(x, a_hi, a_lo, diag)
        x, first, last = rim(part, *halo, a_hi, a_lo)
        halo = exchange(first, last)
    part = own(x, a_hi, a_lo, diag)
    partial_sum = unpack(vals, dest, cells)
    remapped = lax.ppermute(partial_sum, "sec", [(0, 1), (1, 0)])
    out = finish(part, *halo, a_hi, a_lo, remapped, coupling_rate[0], vertical_mix[0])
    return out[None], remapped[None]


def solution(mesh):
    return jax.shard_map(
        per_device,
        mesh=mesh,
        in_specs=(
            P("sec", None, None, "blk"),
            P("sec", None, "blk"),
            P("sec", None, "blk"),
            P("sec", None, "blk"),
            P("sec", None, None, None),
            P("sec", "blk"),
            P("sec", "blk", None),
            P("sec", "blk"),
            P("sec", "blk"),
        ),
        out_specs=(P("sec", None, None, "blk"), P("sec", None, "blk")),
        check_vma=False,
    )
```

```python
import jax
import jax.numpy as jnp
from jax import lax
from jax.experimental import pallas as pl
from jax.experimental.pallas import tpu as pltpu
from jax.sharding import PartitionSpec as P

SUB = 4
RIM = 128
LANE = 128
BF = jnp.bfloat16
F32 = jnp.float32
VMEM = pltpu.VMEM


def dot(a, b):
    return jnp.dot(a, b, preferred_element_type=F32)


def dot_nt(a, b):
    return lax.dot_general(a, b, (((1,), (1,)), ((), ())), preferred_element_type=F32)


def split(x):
    hi = x.astype(BF)
    lo = (x - hi.astype(F32)).astype(BF)
    return hi, lo


def build_kernel(nbr_ref, w_ref, hi_ref, lo_ref, diag_ref):
    rows, cells = hi_ref.shape
    lines = cells // LANE
    slots = nbr_ref.shape[0] // lines
    step = 16
    first = lax.broadcasted_iota(jnp.int32, (step, LANE), 0).astype(F32)

    def body(i, _):
        lanes = pl.ds(pl.multiple_of(i * LANE, LANE), LANE)
        pos, wgt = [], []
        for k in range(slots):
            p = nbr_ref[pl.ds(k * lines + i, 1), :]
            p = jnp.where(p < RIM, p + cells, jnp.where(p < cells + RIM, p - RIM, p))
            pos.append(p)
            wgt.append(w_ref[pl.ds(k * lines + i, 1), :])
        total = wgt[0]
        for k in range(1, slots):
            total = total + wgt[k]
        diag_ref[:, lanes] = 1.0 - total
        for k in range(1, slots):
            for j in range(k):
                same = pos[j] == pos[k]
                wgt[j] = jnp.where(same, wgt[j] + wgt[k], wgt[j])
                pos[k] = jnp.where(same, -1, pos[k])
        whi, wlo = [], []
        for k in range(slots):
            hi = wgt[k].astype(BF).astype(F32)
            whi.append(jnp.broadcast_to(hi, (step, LANE)).astype(BF))
            wlo.append(jnp.broadcast_to(wgt[k] - hi, (step, LANE)).astype(BF))
        for block in range(rows // 256):
            loc = []
            for k in range(slots):
                local = pos[k] - block * 256
                local = jnp.where((local >= 0) & (local < 256), local, -1).astype(F32)
                loc.append(jnp.broadcast_to(local, (step, LANE)).astype(BF))
            for part in range(256 // step):
                row = (first + part * step).astype(BF)
                hi = jnp.zeros((step, LANE), BF)
                lo = jnp.zeros((step, LANE), BF)
                for k in range(slots):
                    here = row == loc[k]
                    hi = jnp.where(here, whi[k], hi)
                    lo = jnp.where(here, wlo[k], lo)
                at = pl.ds(block * 256 + part * step, step)
                hi_ref[at, lanes] = hi
                lo_ref[at, lanes] = lo
        return 0

    lax.fori_loop(0, lines, body, 0)


def params(mb):
    return pltpu.CompilerParams(vmem_limit_bytes=mb << 20)


def whole(count):
    return [pl.BlockSpec(memory_space=VMEM)] * count


def build(nbr, w, cells):
    rows = cells + 2 * RIM
    return pl.pallas_call(
        build_kernel,
        in_specs=whole(2),
        out_specs=whole(3),
        out_shape=[
            jax.ShapeDtypeStruct((rows, cells), BF),
            jax.ShapeDtypeStruct((rows, cells), BF),
            jax.ShapeDtypeStruct((1, cells), F32),
        ],
        compiler_params=params(24),
        name="build",
    )(nbr, w)


def own_kernel(x_ref, hi_ref, lo_ref, diag_ref, out_ref, cat_ref):
    columns, cells = x_ref.shape
    hi, lo = split(x_ref[...])
    cat_ref[0:columns, :] = hi
    cat_ref[columns:, :] = lo
    for c in range(cells // 256):
        at = pl.ds(c * 256, 256)
        both = dot(cat_ref[...], hi_ref[0:cells, at])
        low = dot(cat_ref[0:columns, :], lo_ref[0:cells, at])
        out_ref[:, at] = diag_ref[:, at] * x_ref[:, at] + (both[0:columns] + both[columns:] + low)


def own(x, a_hi, a_lo, diag):
    columns, cells = x.shape
    return pl.pallas_call(
        own_kernel,
        in_specs=whole(4),
        out_specs=whole(1)[0],
        out_shape=jax.ShapeDtypeStruct((columns, cells), F32),
        scratch_shapes=[VMEM((2 * columns, cells), BF)],
        compiler_params=params(24),
        name="own",
    )(x, a_hi, a_lo, diag)


def rim_update(part_ref, low_ref, high_ref, hi_ref, lo_ref, c):
    columns, cells = part_ref.shape
    lo_hi, lo_lo = split(low_ref[...])
    hi_hi, hi_lo = split(high_ref[...])
    top = jnp.concatenate([lo_hi, hi_hi], axis=1)
    rest = jnp.concatenate([lo_lo, hi_lo], axis=1)
    lanes = pl.ds(c * 256, 256)
    rows = pl.ds(cells, 2 * RIM)
    both = dot(jnp.concatenate([top, rest], axis=0), hi_ref[rows, lanes])
    return part_ref[:, lanes] + (both[0:columns] + both[columns:] + dot(top, lo_ref[rows, lanes]))


def rim_kernel(part_ref, low_ref, high_ref, hi_ref, lo_ref, out_ref, first_ref, last_ref):
    count = out_ref.shape[1] // 256
    for c in range(count):
        out = rim_update(part_ref, low_ref, high_ref, hi_ref, lo_ref, c)
        out_ref[:, c * 256 : (c + 1) * 256] = out
        if c == 0:
            first_ref[...] = out[:, 0:RIM]
        if c == count - 1:
            last_ref[...] = out[:, 256 - RIM :]


def rim(part, low, high, a_hi, a_lo):
    columns, cells = part.shape
    return pl.pallas_call(
        rim_kernel,
        in_specs=whole(5),
        out_specs=whole(3),
        out_shape=[
            jax.ShapeDtypeStruct((columns, cells), F32),
            jax.ShapeDtypeStruct((columns, RIM), F32),
            jax.ShapeDtypeStruct((columns, RIM), F32),
        ],
        compiler_params=params(24),
        name="rim",
    )(part, low, high, a_hi, a_lo)


def finish_kernel(
    part_ref, low_ref, high_ref, hi_ref, lo_ref, remapped_ref, rate_ref, mix_ref,
    out_ref, copy_ref,
):
    fields, levels = mix_ref.shape[0], mix_ref.shape[1]
    copy_ref[...] = remapped_ref[...]
    row = lax.broadcasted_iota(jnp.int32, (levels, 256), 0)
    mixes = [split(mix_ref[f]) for f in range(fields)]
    for c in range(part_ref.shape[1] // 256):
        mixed = rim_update(part_ref, low_ref, high_ref, hi_ref, lo_ref, c)
        at = pl.ds(c * 256, 256)
        for f in range(fields):
            mine = mixed[f * levels : (f + 1) * levels]
            top = mine[0:1]
            top = top + rate_ref[f : f + 1, at] * (remapped_ref[f : f + 1, at] - top)
            forced = jnp.where(row == 0, jnp.broadcast_to(top, mine.shape), mine)
            hi, lo = split(forced)
            m_hi, m_lo = mixes[f]
            out_ref[f, :, at] = dot(m_hi, hi) + (dot(m_hi, lo) + dot(m_lo, hi))


def finish(part, low, high, a_hi, a_lo, remapped, rate, mix):
    columns, cells = part.shape
    fields, levels = mix.shape[0], mix.shape[1]
    return pl.pallas_call(
        finish_kernel,
        in_specs=whole(8),
        out_specs=whole(2),
        out_shape=[
            jax.ShapeDtypeStruct((fields, levels, cells), F32),
            jax.ShapeDtypeStruct((fields, cells), F32),
        ],
        compiler_params=params(24),
        name="finish",
    )(part, low, high, a_hi, a_lo, remapped, rate, mix)


def row16(row):
    return jnp.broadcast_to(row, (16, LANE))


def pack_kernel(
    state_ref, source_ref, owner_ref, cell_ref, weight_ref, out_ref,
    tiles_ref, slot_ref, owner_f_ref, piece_ref, hot_ref, rank_ref, left_ref, right_ref, acc_ref,
):
    fields = state_ref.shape[0]
    rows = source_ref.shape[0]
    blocks = out_ref.shape[0] // 16
    chunk = right_ref.shape[1]
    per = chunk // LANE
    groups = blocks // 2
    owner_f_ref[...] = owner_ref[...].astype(F32)
    cell = cell_ref[...]
    piece_ref[0:rows, :] = ((cell // 16) * 16).astype(F32)
    piece_ref[rows:, :] = (cell % 16).astype(F32)
    source = source_ref[...]
    line, lane = source // LANE, source % LANE
    for f in range(fields):
        got = jnp.zeros((rows, LANE), F32)
        for h in range(state_ref.shape[2] // LANE):
            table = jnp.broadcast_to(state_ref[f, 0:1, h * LANE : (h + 1) * LANE], (rows, LANE))
            one = jnp.take_along_axis(table, lane, axis=1, mode="promise_in_bounds")
            got = jnp.where(line == h, one, got)
        got = got * weight_ref[...]
        hi = got.astype(BF).astype(F32)
        tiles_ref[pl.ds(f, rows, stride=2 * fields), :] = hi
        tiles_ref[pl.ds(fields + f, rows, stride=2 * fields), :] = got - hi
    i16 = lax.broadcasted_iota(jnp.int32, (16, LANE), 0).astype(F32)
    i0 = lax.broadcasted_iota(jnp.int32, (LANE, 2 * LANE), 0)
    i1 = lax.broadcasted_iota(jnp.int32, (LANE, 2 * LANE), 1)
    before = jnp.where(i0 < i1, 1.0, 0.0).astype(BF)
    one16 = jnp.ones((16, LANE), BF)
    zero16 = jnp.zeros((16, LANE), BF)
    for r in range(rows):
        who = row16(owner_f_ref[r : r + 1, :]).astype(BF)
        for j in range(blocks // 16):
            here = (i16 + j * 16).astype(BF) == who
            hot_ref[r * blocks + j * 16 : r * blocks + (j + 1) * 16, :] = jnp.where(here, one16, zero16)
    rank_ref[...] = dot(hot_ref[...], before)
    base = jnp.zeros((blocks, LANE), F32)
    for r in range(rows):
        at = pl.ds(r * blocks, blocks)
        hot = hot_ref[at, :].astype(F32)
        slot_ref[r : r + 1, :] = jnp.sum(hot * (rank_ref[at, 0:LANE] + base), axis=0, keepdims=True)
        base = base + rank_ref[at, LANE:]

    acc_ref[...] = jnp.zeros_like(acc_ref)
    eight = jnp.where(i16 < 8, 0.0, 1.0)

    def body(c, _):
        for t in range(per):
            r = c * per + t
            at = pl.ds(t * LANE, LANE)
            one = pl.ds(r, 1)
            tile = tiles_ref[pl.ds(pl.multiple_of(r * 8, 8), 8), :]
            tile = jnp.concatenate([tile, tile], axis=0).astype(BF)
            owner = row16(owner_f_ref[one, :])
            who = (owner - eight).astype(BF)
            for o in range(groups):
                left_ref[o * 16 : (o + 1) * 16, at] = jnp.where(who == 2 * o, tile, zero16)
            who = (owner - i16).astype(BF)
            for part in range(2):
                piece = row16(piece_ref[pl.ds(part * rows + r, 1), :]).astype(BF)
                for o in range(blocks // 16):
                    top = groups * 16 + part * blocks + o * 16
                    left_ref[top : top + 16, at] = jnp.where(who == 16 * o, piece, zero16)
            who = row16(slot_ref[one, :]).astype(BF)
            for o in range(2 * LANE // 16):
                here = (i16 + o * 16).astype(BF) == who
                right_ref[o * 16 : (o + 1) * 16, at] = jnp.where(here, one16, zero16)
        acc_ref[...] += dot_nt(left_ref[...], right_ref[...])
        return 0

    lax.fori_loop(0, rows // per, body, 0)
    low = lax.broadcasted_iota(jnp.int32, (8, LANE), 0) < 4
    for o in range(blocks):
        at = pl.ds(o * 8, 8)
        left, right = acc_ref[at, 0:LANE], acc_ref[at, LANE:]
        left = left + pltpu.roll(left, 4, 0)
        right = right + pltpu.roll(right, 4, 0)
        out_ref[o * 16 : o * 16 + 8, :] = jnp.where(low, left, right)
    top = blocks * 8
    for h in range(2):
        lanes = pl.ds(h * LANE, LANE)
        out_ref[pl.ds(8 + h, blocks, stride=16), :] = (
            acc_ref[top : top + blocks, lanes] + acc_ref[top + blocks :, lanes]
        )


def pack(state, source, owner, cell, weight, blocks):
    fields, levels, cells = state.shape
    rows = source.shape[0]
    chunk = 512
    return pl.pallas_call(
        pack_kernel,
        grid=(1,),
        in_specs=[pl.BlockSpec((fields, 8, cells), lambda i: (0, 0, 0))] + whole(4),
        out_specs=whole(1)[0],
        out_shape=jax.ShapeDtypeStruct((blocks * 16, LANE), F32),
        scratch_shapes=[
            VMEM((rows * 2 * fields, LANE), F32),
            VMEM((rows, LANE), F32),
            VMEM((rows, LANE), F32),
            VMEM((2 * rows, LANE), F32),
            VMEM((rows * blocks, LANE), BF),
            VMEM((rows * blocks, 2 * LANE), F32),
            VMEM((blocks * 10, chunk), BF),
            VMEM((2 * LANE, chunk), BF),
            VMEM((blocks * 10, 2 * LANE), F32),
        ],
        compiler_params=params(20),
        name="pack",
    )(state, source, owner, cell, weight)


def unpack_kernel(in_ref, out_ref, left_ref, right_ref):
    fields, cells = out_ref.shape
    blocks = in_ref.shape[0] // 16
    groups = cells // 256
    chunk = right_ref.shape[1]
    per = chunk // (2 * LANE)
    i16 = lax.broadcasted_iota(jnp.int32, (16, LANE), 0).astype(F32)
    eight = jnp.where(i16 < 8, 0.0, 1.0)
    one16 = jnp.ones((16, LANE), BF)
    zero16 = jnp.zeros((16, LANE), BF)

    def body(c, acc):
        for t in range(2 * per):
            top = pl.multiple_of((c * per + t // 2) * 16, 16)
            at = pl.ds(t * LANE, LANE)
            cell = in_ref[pl.ds(top + 8 + t % 2, 1), :].astype(jnp.int32)
            group = (cell // 256).astype(F32)
            local = row16((cell % 256).astype(F32)).astype(BF)
            vals = in_ref[pl.ds(top, 8), :][(t % 2) * 4 : (t % 2) * 4 + 4]
            hi = vals.astype(BF).astype(F32)
            lo = vals - hi
            tile = jnp.concatenate([hi, lo, hi, lo], axis=0).astype(BF)
            who = (row16(group) - eight).astype(BF)
            for g in range(groups // 2):
                left_ref[g * 16 : (g + 1) * 16, at] = jnp.where(who == 2 * g, tile, zero16)
            for o in range(16):
                here = (i16 + o * 16).astype(BF) == local
                right_ref[o * 16 : (o + 1) * 16, at] = jnp.where(here, one16, zero16)
        return acc + dot_nt(left_ref[...], right_ref[...])

    acc = lax.fori_loop(0, blocks // per, body, jnp.zeros((groups * 8, 256), F32))
    for g in range(groups):
        out_ref[:, g * 256 : (g + 1) * 256] = acc[g * 8 : g * 8 + 4] + acc[g * 8 + 4 : g * 8 + 8]


def unpack(packed, fields, count):
    chunk = 1024
    return pl.pallas_call(
        unpack_kernel,
        in_specs=whole(1),
        out_specs=whole(1)[0],
        out_shape=jax.ShapeDtypeStruct((fields, count), F32),
        scratch_shapes=[VMEM((count // 256 * 8, chunk), BF), VMEM((256, chunk), BF)],
        compiler_params=params(16),
        name="unpack",
    )(packed)


def per_device(
    state, neighbour, edge_weight, coupling_rate, vertical_mix,
    remap_source, remap_owner, remap_cell, remap_weight,
):
    fields, levels, cells = state.shape[1:]
    columns = fields * levels
    blocks = lax.axis_size("blk")
    forward = [(i, (i + 1) % blocks) for i in range(blocks)]
    backward = [(b, a) for a, b in forward]

    def lines(x):
        return x.reshape(-1, LANE)

    def exchange(first, last):
        low = lax.ppermute(last, "blk", forward)
        high = lax.ppermute(first, "blk", backward)
        return low, high

    x = state.reshape(columns, cells)
    halo = exchange(x[:, :RIM], x[:, cells - RIM :])
    packed = pack(
        state[0], lines(remap_source), lines(remap_owner), lines(remap_cell),
        lines(remap_weight), blocks,
    )
    packed = lax.all_to_all(packed.reshape(blocks, 16, LANE), "blk", 0, 0, tiled=True)
    a_hi, a_lo, diag = build(lines(neighbour), lines(edge_weight), cells)
    for step in range(SUB - 1):
        part = own(x, a_hi, a_lo, diag)
        x, first, last = rim(part, *halo, a_hi, a_lo)
        halo = exchange(first, last)
    part = own(x, a_hi, a_lo, diag)
    partial_sum = unpack(packed.reshape(blocks * 16, LANE), fields, cells)
    remapped = lax.ppermute(partial_sum, "sec", [(0, 1), (1, 0)])
    out, remapped = finish(part, *halo, a_hi, a_lo, remapped, coupling_rate[0], vertical_mix[0])
    return out[None], remapped[None]


def solution(mesh):
    return jax.shard_map(
        per_device,
        mesh=mesh,
        in_specs=(
            P("sec", None, None, "blk"),
            P("sec", None, "blk"),
            P("sec", None, "blk"),
            P("sec", None, "blk"),
            P("sec", None, None, None),
            P("sec", "blk"),
            P("sec", "blk", None),
            P("sec", "blk"),
            P("sec", "blk"),
        ),
        out_specs=(P("sec", None, None, "blk"), P("sec", None, "blk")),
        check_vma=False,
    )
```

```python
import jax
import jax.numpy as jnp
from jax import lax
from jax.experimental import pallas as pl
from jax.experimental.pallas import tpu as pltpu
from jax.sharding import PartitionSpec as P

SUB = 4
RIM = 128
LANE = 128
BF = jnp.bfloat16
F32 = jnp.float32
VMEM = pltpu.VMEM


def dot(a, b):
    return jnp.dot(a, b, preferred_element_type=F32)


def dot_nt(a, b):
    return lax.dot_general(a, b, (((1,), (1,)), ((), ())), preferred_element_type=F32)


def split(x):
    hi = x.astype(BF)
    lo = (x - hi.astype(F32)).astype(BF)
    return hi, lo


def build_tile(nbr_ref, w_ref, hi_ref, lo_ref, diag_ref, i, to):
    rows = hi_ref.shape[0]
    cells = rows - 2 * RIM
    lines = cells // LANE
    slots = nbr_ref.shape[0] // lines
    step = 16
    first = lax.broadcasted_iota(jnp.int32, (step, LANE), 0).astype(F32)
    lanes = pl.ds(to * LANE if isinstance(to, int) else pl.multiple_of(to * LANE, LANE), LANE)
    pos, wgt = [], []
    for k in range(slots):
        p = nbr_ref[pl.ds(k * lines + i, 1), :]
        p = jnp.where(p < RIM, p + cells, jnp.where(p < cells + RIM, p - RIM, p))
        pos.append(p)
        wgt.append(w_ref[pl.ds(k * lines + i, 1), :])
    total = wgt[0]
    for k in range(1, slots):
        total = total + wgt[k]
    diag_ref[:, lanes] = 1.0 - total
    for k in range(1, slots):
        for j in range(k):
            same = pos[j] == pos[k]
            wgt[j] = jnp.where(same, wgt[j] + wgt[k], wgt[j])
            pos[k] = jnp.where(same, -1, pos[k])
    whi, wlo = [], []
    for k in range(slots):
        hi = wgt[k].astype(BF).astype(F32)
        whi.append(jnp.broadcast_to(hi, (step, LANE)).astype(BF))
        wlo.append(jnp.broadcast_to(wgt[k] - hi, (step, LANE)).astype(BF))
    for block in range(rows // 256):
        loc = []
        for k in range(slots):
            local = pos[k] - block * 256
            local = jnp.where((local >= 0) & (local < 256), local, -1).astype(F32)
            loc.append(jnp.broadcast_to(local, (step, LANE)).astype(BF))
        for part in range(256 // step):
            row = (first + part * step).astype(BF)
            hi = jnp.zeros((step, LANE), BF)
            lo = jnp.zeros((step, LANE), BF)
            for k in range(slots):
                here = row == loc[k]
                hi = jnp.where(here, whi[k], hi)
                lo = jnp.where(here, wlo[k], lo)
            at = pl.ds(block * 256 + part * step, step)
            hi_ref[at, lanes] = hi
            lo_ref[at, lanes] = lo


def fetch(pairs, sems):
    copies = [pltpu.make_async_copy(a, b, sems.at[n]) for n, (a, b) in enumerate(pairs)]
    for copy in copies:
        copy.start()
    return copies


def odd_block():
    return lax.axis_index("blk") % 2 == 1


def sides(pair_ref, other_ref):
    odd = odd_block()
    pair, other = pair_ref[...], other_ref[...]
    return jnp.where(odd, pair, other), jnp.where(odd, other, pair)


def send(first, last, pair_ref, other_ref):
    odd = odd_block()
    pair_ref[...] = jnp.where(odd, first, last)
    other_ref[...] = jnp.where(odd, last, first)


def fill_cat(cat_ref, x_ref, pair_ref, other_ref):
    columns, cells = x_ref.shape
    low, high = sides(pair_ref, other_ref)
    for value, at in (
        (x_ref[...], pl.ds(0, cells)),
        (low, pl.ds(cells, RIM)),
        (high, pl.ds(cells + RIM, RIM)),
    ):
        hi, lo = split(value)
        cat_ref[0:columns, at] = hi
        cat_ref[columns:, at] = lo


def product(cat_ref, hi_ref, lo_ref, rows, lanes):
    columns = cat_ref.shape[0] // 2
    at = pl.ds(0, rows)
    both = dot(cat_ref[:, at], hi_ref[at, lanes])
    low = dot(cat_ref[0:columns, at], lo_ref[at, lanes])
    return both[0:columns] + both[columns:] + low


def edge_kernel(
    nbr_hbm, w_hbm, x_hbm, pair_ref, other_ref, pair_out, other_out,
    nbr_ref, w_ref, x_ref, hi_ref, lo_ref, diag_ref, cat_ref, sems,
):
    copies = fetch(((nbr_hbm, nbr_ref), (w_hbm, w_ref), (x_hbm, x_ref)), sems)
    rows, cells = hi_ref.shape[0], x_ref.shape[1]
    copies[0].wait()
    copies[1].wait()
    last = cells // LANE - 1
    build_tile(nbr_ref, w_ref, hi_ref, lo_ref, diag_ref, 0, 0)
    build_tile(nbr_ref, w_ref, hi_ref, lo_ref, diag_ref, last, 1)
    copies[2].wait()
    fill_cat(cat_ref, x_ref, pair_ref, other_ref)
    ends = []
    for n, i in enumerate((0, last)):
        lanes, mine = pl.ds(i * LANE, LANE), pl.ds(n * LANE, LANE)
        ends.append(
            diag_ref[:, mine] * x_ref[:, lanes] + product(cat_ref, hi_ref, lo_ref, rows, mine)
        )
    send(*ends, pair_out, other_out)


def main_kernel(
    nbr_hbm, w_hbm, x_hbm, pair_ref, other_ref,
    hi_ref, lo_ref, diag_ref, out_ref, nbr_ref, w_ref, x_ref, cat_ref, y_ref, sems,
):
    copies = fetch(((nbr_hbm, nbr_ref), (w_hbm, w_ref), (x_hbm, x_ref)), sems)
    rows, cells = hi_ref.shape
    columns = x_ref.shape[0]
    copies[0].wait()
    copies[1].wait()

    def body(i, _):
        build_tile(nbr_ref, w_ref, hi_ref, lo_ref, diag_ref, i, i)
        return 0

    lax.fori_loop(0, cells // LANE, body, 0)
    copies[2].wait()
    fill_cat(cat_ref, x_ref, pair_ref, other_ref)
    for c in range(cells // 256):
        at = pl.ds(c * 256, 256)
        y_ref[:, at] = diag_ref[:, at] * x_ref[:, at] + product(cat_ref, hi_ref, lo_ref, rows, at)
    hi, lo = split(y_ref[...])
    cat_ref[0:columns, 0:cells] = hi
    cat_ref[columns:, 0:cells] = lo
    for c in range(cells // 256):
        at = pl.ds(c * 256, 256)
        out_ref[:, at] = diag_ref[:, at] * y_ref[:, at] + product(cat_ref, hi_ref, lo_ref, cells, at)


def params(mb):
    return pltpu.CompilerParams(vmem_limit_bytes=mb << 20)


def whole(count):
    return [pl.BlockSpec(memory_space=VMEM)] * count


HBM = pl.BlockSpec(memory_space=pltpu.HBM)


def operator_shapes(cells):
    rows = cells + 2 * RIM
    return [
        jax.ShapeDtypeStruct((rows, cells), BF),
        jax.ShapeDtypeStruct((rows, cells), BF),
        jax.ShapeDtypeStruct((1, cells), F32),
    ]


def pinned(*arrays):
    return [pltpu.with_memory_space_constraint(x, pltpu.HBM) for x in arrays]


def edge(nbr, w, x, low, high):
    columns, cells = x.shape
    rows = cells + 2 * RIM
    return pl.pallas_call(
        edge_kernel,
        in_specs=[HBM] * 3 + whole(2),
        out_specs=whole(2),
        out_shape=[jax.ShapeDtypeStruct((columns, RIM), F32)] * 2,
        scratch_shapes=[
            VMEM(nbr.shape, nbr.dtype),
            VMEM(w.shape, w.dtype),
            VMEM((columns, cells), F32),
            VMEM((rows, 2 * LANE), BF),
            VMEM((rows, 2 * LANE), BF),
            VMEM((1, 2 * LANE), F32),
            VMEM((2 * columns, rows), BF),
            pltpu.SemaphoreType.DMA((3,)),
        ],
        compiler_params=params(24),
        name="edge",
    )(*pinned(nbr, w, x), low, high)


def main(nbr, w, x, low, high):
    columns, cells = x.shape
    return pl.pallas_call(
        main_kernel,
        in_specs=[HBM] * 3 + whole(2),
        out_specs=whole(4),
        out_shape=operator_shapes(cells) + [jax.ShapeDtypeStruct((columns, cells), F32)],
        scratch_shapes=[
            VMEM(nbr.shape, nbr.dtype),
            VMEM(w.shape, w.dtype),
            VMEM((columns, cells), F32),
            VMEM((2 * columns, cells + 2 * RIM), BF),
            VMEM((columns, cells), F32),
            pltpu.SemaphoreType.DMA((3,)),
        ],
        compiler_params=params(24),
        name="main",
    )(*pinned(nbr, w, x), low, high)


def own_kernel(x_ref, hi_ref, lo_ref, diag_ref, out_ref, cat_ref):
    columns, cells = x_ref.shape
    hi, lo = split(x_ref[...])
    cat_ref[0:columns, :] = hi
    cat_ref[columns:, :] = lo
    for c in range(cells // 256):
        at = pl.ds(c * 256, 256)
        both = dot(cat_ref[...], hi_ref[0:cells, at])
        low = dot(cat_ref[0:columns, :], lo_ref[0:cells, at])
        out_ref[:, at] = diag_ref[:, at] * x_ref[:, at] + (both[0:columns] + both[columns:] + low)


def own(x, a_hi, a_lo, diag):
    columns, cells = x.shape
    return pl.pallas_call(
        own_kernel,
        in_specs=whole(4),
        out_specs=whole(1)[0],
        out_shape=jax.ShapeDtypeStruct((columns, cells), F32),
        scratch_shapes=[VMEM((2 * columns, cells), BF)],
        compiler_params=params(24),
        name="own",
    )(x, a_hi, a_lo, diag)


def rim_update(part_ref, pair_ref, other_ref, hi_ref, lo_ref, c):
    columns, cells = part_ref.shape
    low, high = sides(pair_ref, other_ref)
    lo_hi, lo_lo = split(low)
    hi_hi, hi_lo = split(high)
    top = jnp.concatenate([lo_hi, hi_hi], axis=1)
    rest = jnp.concatenate([lo_lo, hi_lo], axis=1)
    lanes = pl.ds(c * 256, 256)
    rows = pl.ds(cells, 2 * RIM)
    both = dot(jnp.concatenate([top, rest], axis=0), hi_ref[rows, lanes])
    return part_ref[:, lanes] + (both[0:columns] + both[columns:] + dot(top, lo_ref[rows, lanes]))


def rim_kernel(part_ref, pair_ref, other_ref, hi_ref, lo_ref, out_ref, pair_out, other_out):
    count = out_ref.shape[1] // 256
    for c in range(count):
        out = rim_update(part_ref, pair_ref, other_ref, hi_ref, lo_ref, c)
        out_ref[:, c * 256 : (c + 1) * 256] = out
        if c == 0:
            first = out[:, 0:RIM]
        if c == count - 1:
            send(first, out[:, 256 - RIM :], pair_out, other_out)


def rim(part, low, high, a_hi, a_lo):
    columns, cells = part.shape
    return pl.pallas_call(
        rim_kernel,
        in_specs=whole(5),
        out_specs=whole(3),
        out_shape=[
            jax.ShapeDtypeStruct((columns, cells), F32),
            jax.ShapeDtypeStruct((columns, RIM), F32),
            jax.ShapeDtypeStruct((columns, RIM), F32),
        ],
        compiler_params=params(24),
        name="rim",
    )(part, low, high, a_hi, a_lo)


def finish_kernel(
    part_ref, pair_ref, other_ref, hi_ref, lo_ref, remapped_ref, rate_ref, mix_ref,
    out_ref, copy_ref,
):
    fields, levels = mix_ref.shape[0], mix_ref.shape[1]
    copy_ref[...] = remapped_ref[...]
    row = lax.broadcasted_iota(jnp.int32, (levels, 256), 0)
    mixes = [split(mix_ref[f]) for f in range(fields)]
    for c in range(part_ref.shape[1] // 256):
        mixed = rim_update(part_ref, pair_ref, other_ref, hi_ref, lo_ref, c)
        at = pl.ds(c * 256, 256)
        for f in range(fields):
            mine = mixed[f * levels : (f + 1) * levels]
            top = mine[0:1]
            top = top + rate_ref[f : f + 1, at] * (remapped_ref[f : f + 1, at] - top)
            forced = jnp.where(row == 0, jnp.broadcast_to(top, mine.shape), mine)
            hi, lo = split(forced)
            m_hi, m_lo = mixes[f]
            out_ref[f, :, at] = dot(m_hi, hi) + (dot(m_hi, lo) + dot(m_lo, hi))


def finish(part, low, high, a_hi, a_lo, remapped, rate, mix):
    columns, cells = part.shape
    fields, levels = mix.shape[0], mix.shape[1]
    return pl.pallas_call(
        finish_kernel,
        in_specs=whole(8),
        out_specs=whole(2),
        out_shape=[
            jax.ShapeDtypeStruct((fields, levels, cells), F32),
            jax.ShapeDtypeStruct((fields, cells), F32),
        ],
        compiler_params=params(24),
        name="finish",
    )(part, low, high, a_hi, a_lo, remapped, rate, mix)


def row16(row):
    return jnp.broadcast_to(row, (16, LANE))


def pack_kernel(
    state_hbm, source_hbm, owner_hbm, cell_hbm, weight_hbm, out_ref,
    state_ref, source_ref, owner_ref, cell_ref, weight_ref, sems,
    tiles_ref, slot_ref, owner_f_ref, piece_ref, hot_ref, rank_ref, left_a, left_b, right_a, right_b, acc_ref,
):
    copies = fetch(
        (
            (owner_hbm, owner_ref),
            (source_hbm, source_ref),
            (cell_hbm, cell_ref),
            (weight_hbm, weight_ref),
            (state_hbm.at[:, pl.ds(0, 8), :], state_ref),
        ),
        sems,
    )
    for copy in copies:
        copy.wait()
    fields = state_ref.shape[0]
    rows = source_ref.shape[0]
    blocks = out_ref.shape[0] // 16
    chunk = right_a.shape[1]
    per = chunk // LANE
    groups = blocks // 2
    owner_f_ref[...] = owner_ref[...].astype(F32)
    cell = cell_ref[...]
    piece_ref[0:rows, :] = ((cell // 16) * 16).astype(F32)
    piece_ref[rows:, :] = (cell % 16).astype(F32)
    source = source_ref[...]
    line, lane = source // LANE, source % LANE
    for f in range(fields):
        got = jnp.zeros((rows, LANE), F32)
        for h in range(state_ref.shape[2] // LANE):
            table = jnp.broadcast_to(state_ref[f, 0:1, h * LANE : (h + 1) * LANE], (rows, LANE))
            one = jnp.take_along_axis(table, lane, axis=1, mode="promise_in_bounds")
            got = jnp.where(line == h, one, got)
        got = got * weight_ref[...]
        hi = got.astype(BF).astype(F32)
        tiles_ref[pl.ds(f, rows, stride=2 * fields), :] = hi
        tiles_ref[pl.ds(fields + f, rows, stride=2 * fields), :] = got - hi
    i16 = lax.broadcasted_iota(jnp.int32, (16, LANE), 0).astype(F32)
    i0 = lax.broadcasted_iota(jnp.int32, (LANE, 2 * LANE), 0)
    i1 = lax.broadcasted_iota(jnp.int32, (LANE, 2 * LANE), 1)
    before = jnp.where(i0 < i1, 1.0, 0.0).astype(BF)
    one16 = jnp.ones((16, LANE), BF)
    zero16 = jnp.zeros((16, LANE), BF)
    for r in range(rows):
        who = row16(owner_f_ref[r : r + 1, :]).astype(BF)
        for j in range(blocks // 16):
            here = (i16 + j * 16).astype(BF) == who
            hot_ref[r * blocks + j * 16 : r * blocks + (j + 1) * 16, :] = jnp.where(here, one16, zero16)
    rank_ref[...] = dot(hot_ref[...], before)
    base = jnp.zeros((blocks, LANE), F32)
    for r in range(rows):
        at = pl.ds(r * blocks, blocks)
        hot = hot_ref[at, :].astype(F32)
        slot_ref[r : r + 1, :] = jnp.sum(hot * (rank_ref[at, 0:LANE] + base), axis=0, keepdims=True)
        base = base + rank_ref[at, LANE:]

    eight = jnp.where(i16 < 8, 0.0, 1.0)
    for c in range(rows // per):
        left_ref, right_ref = ((left_a, right_a), (left_b, right_b))[c % 2]
        for t in range(per):
            r = c * per + t
            at = pl.ds(t * LANE, LANE)
            tile = tiles_ref[r * 8 : r * 8 + 8, :]
            tile = jnp.concatenate([tile, tile], axis=0).astype(BF)
            owner = row16(owner_f_ref[r : r + 1, :])
            who = (owner - eight).astype(BF)
            for o in range(groups):
                left_ref[o * 16 : (o + 1) * 16, at] = jnp.where(who == 2 * o, tile, zero16)
            who = (owner - i16).astype(BF)
            for part in range(2):
                piece = row16(piece_ref[part * rows + r : part * rows + r + 1, :]).astype(BF)
                for o in range(blocks // 16):
                    top = groups * 16 + part * blocks + o * 16
                    left_ref[top : top + 16, at] = jnp.where(who == 16 * o, piece, zero16)
            who = row16(slot_ref[r : r + 1, :]).astype(BF)
            for o in range(2 * LANE // 16):
                here = (i16 + o * 16).astype(BF) == who
                right_ref[o * 16 : (o + 1) * 16, at] = jnp.where(here, one16, zero16)
        more = dot_nt(left_ref[...], right_ref[...])
        acc_ref[...] = more if c == 0 else acc_ref[...] + more

    low = lax.broadcasted_iota(jnp.int32, (8, LANE), 0) < 4
    for o in range(blocks):
        at = pl.ds(o * 8, 8)
        left, right = acc_ref[at, 0:LANE], acc_ref[at, LANE:]
        left = left + pltpu.roll(left, 4, 0)
        right = right + pltpu.roll(right, 4, 0)
        out_ref[o * 16 : o * 16 + 8, :] = jnp.where(low, left, right)
    top = blocks * 8
    for h in range(2):
        lanes = pl.ds(h * LANE, LANE)
        out_ref[pl.ds(8 + h, blocks, stride=16), :] = (
            acc_ref[top : top + blocks, lanes] + acc_ref[top + blocks :, lanes]
        )


def pack(state, source, owner, cell, weight, blocks):
    fields, levels, cells = state.shape
    rows = source.shape[0]
    chunk = 1024
    return pl.pallas_call(
        pack_kernel,
        in_specs=[HBM] * 5,
        out_specs=whole(1)[0],
        out_shape=jax.ShapeDtypeStruct((blocks * 16, LANE), F32),
        scratch_shapes=[
            VMEM((fields, 8, cells), F32),
            VMEM((rows, LANE), jnp.int32),
            VMEM((rows, LANE), jnp.int32),
            VMEM((rows, LANE), jnp.int32),
            VMEM((rows, LANE), F32),
            pltpu.SemaphoreType.DMA((5,)),
            VMEM((rows * 2 * fields, LANE), F32),
            VMEM((rows, LANE), F32),
            VMEM((rows, LANE), F32),
            VMEM((2 * rows, LANE), F32),
            VMEM((rows * blocks, LANE), BF),
            VMEM((rows * blocks, 2 * LANE), F32),
            VMEM((blocks * 10, chunk), BF),
            VMEM((blocks * 10, chunk), BF),
            VMEM((2 * LANE, chunk), BF),
            VMEM((2 * LANE, chunk), BF),
            VMEM((blocks * 10, 2 * LANE), F32),
        ],
        compiler_params=params(20),
        name="pack",
    )(*pinned(state, source, owner, cell, weight))


def unpack_kernel(in_ref, out_ref, left_ref, right_ref):
    fields, cells = out_ref.shape
    blocks = in_ref.shape[0] // 16
    groups = cells // 256
    i16 = lax.broadcasted_iota(jnp.int32, (16, LANE), 0).astype(F32)
    eight = jnp.where(i16 < 8, 0.0, 1.0)
    one16 = jnp.ones((16, LANE), BF)
    zero16 = jnp.zeros((16, LANE), BF)
    per = 4

    def body(c, _):
        for t in range(2 * per):
            top = pl.multiple_of((c * per + t // 2) * 16, 16)
            at = pl.ds(pl.multiple_of((c * 2 * per + t) * LANE, LANE), LANE)
            cell = in_ref[pl.ds(top + 8 + t % 2, 1), :].astype(jnp.int32)
            group = (cell // 256).astype(F32)
            local = row16((cell % 256).astype(F32)).astype(BF)
            vals = in_ref[pl.ds(top, 8), :][(t % 2) * 4 : (t % 2) * 4 + 4]
            hi = vals.astype(BF).astype(F32)
            lo = vals - hi
            tile = jnp.concatenate([hi, lo, hi, lo], axis=0).astype(BF)
            who = (row16(group) - eight).astype(BF)
            for g in range(groups // 2):
                left_ref[g * 16 : (g + 1) * 16, at] = jnp.where(who == 2 * g, tile, zero16)
            for o in range(16):
                here = (i16 + o * 16).astype(BF) == local
                right_ref[o * 16 : (o + 1) * 16, at] = jnp.where(here, one16, zero16)
        return 0

    lax.fori_loop(0, blocks // per, body, 0)
    acc = dot_nt(left_ref[...], right_ref[...])
    for g in range(groups):
        out_ref[:, g * 256 : (g + 1) * 256] = acc[g * 8 : g * 8 + 4] + acc[g * 8 + 4 : g * 8 + 8]


def unpack(packed, fields, count):
    chunk = packed.shape[0] // 8 * LANE
    return pl.pallas_call(
        unpack_kernel,
        in_specs=whole(1),
        out_specs=whole(1)[0],
        out_shape=jax.ShapeDtypeStruct((fields, count), F32),
        scratch_shapes=[VMEM((count // 256 * 8, chunk), BF), VMEM((256, chunk), BF)],
        compiler_params=params(16),
        name="unpack",
    )(packed)


def per_device(
    state, neighbour, edge_weight, coupling_rate, vertical_mix,
    remap_source, remap_owner, remap_cell, remap_weight,
):
    fields, levels, cells = state.shape[1:]
    columns = fields * levels
    blocks = lax.axis_size("blk")
    pairs = [(i, i ^ 1) for i in range(blocks)]
    others = [(i, (i + 1 if i % 2 else i - 1) % blocks) for i in range(blocks)]

    def lines(x):
        return x.reshape(-1, LANE)

    def exchange(to_pair, to_other):
        return lax.ppermute(to_pair, "blk", pairs), lax.ppermute(to_other, "blk", others)

    x = state.reshape(columns, cells)
    nbr, weight = lines(neighbour), lines(edge_weight)
    odd = lax.axis_index("blk") % 2 == 1
    first, last = x[:, :RIM], x[:, cells - RIM :]
    start = exchange(jnp.where(odd, first, last), jnp.where(odd, last, first))
    packed = pack(
        state[0], lines(remap_source), lines(remap_owner), lines(remap_cell),
        lines(remap_weight), blocks,
    )
    packed = lax.all_to_all(packed.reshape(blocks, 16, LANE), "blk", 0, 0, tiled=True)
    halo = exchange(*edge(nbr, weight, x, *start))
    packed, nbr = lax.optimization_barrier((packed, nbr))
    a_hi, a_lo, diag, part = main(nbr, weight, x, *start)
    for step in range(1, SUB - 1):
        x, *ends = rim(part, *halo, a_hi, a_lo)
        halo = exchange(*ends)
        part = own(x, a_hi, a_lo, diag)
    partial_sum = unpack(packed.reshape(blocks * 16, LANE), fields, cells)
    remapped = lax.ppermute(partial_sum, "sec", [(0, 1), (1, 0)])
    out, remapped = finish(part, *halo, a_hi, a_lo, remapped, coupling_rate[0], vertical_mix[0])
    return out[None], remapped[None]


def solution(mesh):
    return jax.shard_map(
        per_device,
        mesh=mesh,
        in_specs=(
            P("sec", None, None, "blk"),
            P("sec", None, "blk"),
            P("sec", None, "blk"),
            P("sec", None, "blk"),
            P("sec", None, None, None),
            P("sec", "blk"),
            P("sec", "blk", None),
            P("sec", "blk"),
            P("sec", "blk"),
        ),
        out_specs=(P("sec", None, None, "blk"), P("sec", None, "blk")),
        check_vma=False,
    )
```
